32 devices in a mesh: ind: 4 (over x, core), mark: 4 (over z), chip: 2 (over y).
Axes of the slice: x: 2, y: 2, z: 4, core: 2. Of those that a mesh axis runs over, the one named last changes fastest.
Arguments:
- genotypes: bfloat16 [8192, 8192], P(('ind', 'chip'), 'mark'), may hold values from -0.1875 to 0.1875
- residual: float32 [8192, 1024], P(('ind', 'chip'), 'mark'), as said below
- posterior_inverse: bfloat16 [8, 1024, 1024], P('mark'), as said below
- gibbs_noise: bfloat16 [4, 8192, 256], P(None, 'mark'), may hold values from -6 to 6
- visit_order: int32 [4, 4, 2], P(None, 'mark'), may hold values from 0 to 1, each once within a row
Outputs:
- residual_after: float32 [8192, 1024], P(('ind', 'chip'), 'mark')
- effect_changes: float32 [4, 8192, 256], P(None, 'mark')
The draws below stay inside these ranges and needn't reach their ends.
Inputs may be any that keep to these rules, and one draw needn't show every extreme that they name: `visit_order`: each row names each of the 2 marker blocks of one cycle position once. `residual`: finite real values. `posterior_inverse`: the diagonal entries are positive.
All inputs are finite; a program needn't handle non-finite values.
Results may differ from the reference program's by a relative error of at most 0.005.
Values sent between devices are 32-bit elements; how exact they have to be, the bound alone decides.
A program may use at most 128 MiB of HBM per device.

```python
import math
import jax
import jax.numpy as jnp
from jax import lax

MB = 1024
TB = 256
BLK_DEV = 2
TRAITS = 1024
STOPS = 4
MBLOCKS = 8
MARKERS = 8192
INDIV = 8192
N_MARK = 4


def draw_residual(key, part):
    first, second, third = jax.random.split(jax.random.fold_in(key, 11), 3)
    rows = jnp.arange(INDIV, dtype=jnp.float32) / INDIV
    row_scale = jnp.exp(jnp.log(3.0) * rows + jax.random.uniform(first, (INDIV,), jnp.float32, -1.15, 1.15))
    col_scale = jnp.exp(jax.random.uniform(second, (TRAITS,), jnp.float32, -1.15, 1.15))
    base = jnp.clip(jax.random.normal(third, (INDIV, TRAITS), jnp.float32), -6.0, 6.0)
    return (0.3 * base * row_scale[:, None] * col_scale[None, :]).astype(jnp.float32)


def draw_posterior_inverse(key, part):
    first, second = jax.random.split(jax.random.fold_in(key, 23), 2)
    diagonal = jax.random.uniform(first, (MBLOCKS, MB), jnp.float32, 0.4, 0.8)
    offdiag = jax.random.normal(second, (MBLOCKS, MB, MB), jnp.float32) * (0.15 / math.sqrt(MB))
    matrix = offdiag * (1.0 - jnp.eye(MB, dtype=jnp.float32))[None] + jnp.eye(MB, dtype=jnp.float32)[None] * diagonal[:, :, None]
    return (matrix * MB).astype(jnp.bfloat16)


def steps_of(key, dims, cuts, low, largest):
    def one(axis_at, parts):
        steps = jax.random.uniform(jax.random.fold_in(jax.random.fold_in(key, 6), axis_at), (parts,), jnp.float32, low / len(cuts), largest / len(cuts))
        return jnp.repeat(jnp.exp(steps), dims[axis_at] // parts).reshape((-1,) + (1,) * (len(dims) - axis_at - 1))

    gain = one(*cuts[0])
    for cut in cuts[1:]:
        gain = gain * one(*cut)
    return gain


def gaussian(own_key, shape, scale, limit, cuts=(), held_as=jnp.bfloat16):
    gain = steps_of(own_key, shape, cuts, -0.22, 0.18) if cuts else 1.0
    values = jax.random.normal(own_key, shape, jnp.float32) * scale * gain
    return jnp.minimum(jnp.maximum(values, -limit), limit).astype(held_as)


def setup_inputs(seed: int = 0) -> dict:
    keys = jax.random.split(jax.random.key(seed), 6)
    return {
        "genotypes": gaussian(keys[0], (INDIV, MARKERS), MB ** -0.5, 0.1875, ((0, 8), (1, 4))),
        "residual": draw_residual(jax.random.fold_in(keys[5], 71), 0),
        "posterior_inverse": draw_posterior_inverse(jax.random.fold_in(keys[5], 71), 0),
        "gibbs_noise": gaussian(keys[3], (STOPS, MARKERS, TB), 1.0, 6.0, ((1, 4),)),
        "visit_order": jax.vmap(lambda own: jax.random.permutation(own, BLK_DEV))(jax.random.split(keys[4], STOPS * N_MARK)).reshape((STOPS, N_MARK, BLK_DEV)).astype(jnp.int32),
    }


epsilon = 1e-05

def reference(genotypes, residual, posterior_inverse, gibbs_noise, visit_order):
    current_all = residual
    change_list = []
    for stop_idx in range(STOPS):
        stop_changes = jnp.zeros((MARKERS, TB), jnp.float32)
        for cycle_pos in range(N_MARK):
            trait_blk = (cycle_pos - stop_idx) % N_MARK
            current = current_all[:, trait_blk * TB:(trait_blk + 1) * TB]
            for visit_pos in range(BLK_DEV):
                local_blk = visit_order[stop_idx, cycle_pos, visit_pos].astype(jnp.int32)
                global_blk = (local_blk + cycle_pos * BLK_DEV).astype(jnp.int32)
                columns = lax.dynamic_slice_in_dim(genotypes, (global_blk * MB).astype(jnp.int32), MB, 1)
                scores = lax.dot_general(columns, current.astype(jnp.bfloat16), (((0,), (0,)), ((), ())), preferred_element_type=jnp.float32)
                spread = lax.optimization_barrier(jnp.sum(current * current, axis=0)) / INDIV
                inverse = lax.dynamic_index_in_dim(posterior_inverse, global_blk, 0, keepdims=False)
                scaled = (scores / INDIV).astype(jnp.bfloat16)
                mean_part = jnp.dot(inverse, scaled, preferred_element_type=jnp.float32)
                diag_part = jnp.diagonal(inverse).astype(jnp.float32)
                start_row = (cycle_pos * BLK_DEV + visit_pos) * MB
                noise_rows = gibbs_noise[stop_idx, start_row:start_row + MB, :].astype(jnp.float32)
                change = mean_part + jnp.sqrt(diag_part[:, None] * (spread[None, :] + epsilon) / INDIV) * noise_rows
                stop_changes = lax.dynamic_update_slice_in_dim(stop_changes, change, (global_blk * MB).astype(jnp.int32), 0)
                current = current - jnp.dot(columns, change.astype(jnp.bfloat16), preferred_element_type=jnp.float32)
            current_all = current_all.at[:, trait_blk * TB:(trait_blk + 1) * TB].set(current)
        change_list.append(stop_changes)
    return (current_all, jnp.stack(change_list))
```

```python
import functools

import jax
import jax.numpy as jnp
from jax import lax
from jax.experimental import pallas as pl
from jax.experimental.pallas import tpu as pltpu
from jax.sharding import PartitionSpec as P

epsilon = 1e-05
MESH = pl.DeviceIdType.MESH
CHUNKS = 4
NT = (((1,), (1,)), ((), ()))


def kernel(
    cfg,
    order_ref,
    geno_ref,
    resid_ref,
    inv_ref,
    droot_ref,
    noise_ref,
    after_ref,
    change_ref,
    ebuf,
    part,
    r1,
    r2,
    full,
    scaled,
    stash,
    p1s,
    p1r,
    p2s,
    p2r,
    p3s,
    p3r,
    p4s,
    zs,
    zr,
):
    n_ind, n_mark, n_chip, chunks, stops, count, block, rows, lanes, sq_rows = cfg
    quads = n_ind // 2 * n_chip
    tc = ebuf.shape[2]
    lane_blocks = block // lanes
    sq_groups = tc // sq_rows
    ind = lax.axis_index("ind")
    mark = lax.axis_index("mark")
    y = lax.axis_index("chip")
    core = lax.rem(ind, 2)
    other = 1 - core
    q = lax.div(ind, 2) * n_chip + y
    partner = {"ind": ind + 1 - 2 * core}
    nxt = {"mark": lax.rem(mark + 1, n_mark)}
    prv = {"mark": lax.rem(mark + n_mark - 1, n_mark)}

    def chip_at(r):
        qq = lax.rem(q + r, quads)
        return qq, {"ind": lax.div(qq, n_chip) * 2 + core, "chip": lax.rem(qq, n_chip)}

    barrier = pltpu.get_barrier_semaphore()
    pl.semaphore_signal(barrier, inc=1, device_id=partner, device_id_type=MESH)
    pl.semaphore_signal(barrier, inc=1, device_id=nxt, device_id_type=MESH)
    pl.semaphore_signal(barrier, inc=1, device_id=prv, device_id_type=MESH)
    for r in range(1, quads):
        pl.semaphore_signal(barrier, inc=1, device_id=chip_at(r)[1], device_id_type=MESH)

    for c in range(chunks):
        ebuf[0, c] = resid_ref[c]
    pl.semaphore_wait(barrier, quads + 2)

    def copy(src, dst, ssem, rsem, dev):
        return pltpu.make_async_remote_copy(
            src_ref=src, dst_ref=dst, send_sem=ssem, recv_sem=rsem, device_id=dev, device_id_type=MESH
        )

    def hop(stop, c):
        return copy(ebuf.at[stop, c], ebuf.at[stop + 1, c], zs.at[stop, c], zr.at[stop, c], nxt)

    def pair(c):
        return copy(part.at[c, other], r1.at[c], p1s.at[c], p1r.at[c], partner)

    def spread_out(c, r):
        qq, dev = chip_at(r)
        return copy(part.at[c, core, qq], r2.at[c, q], p2s.at[c, qq], p2r.at[c, q], dev)

    def arrived2(c, r):
        qq, dev = chip_at(r)
        return copy(part.at[c, core, qq], r2.at[c, qq], p2s.at[c, qq], p2r.at[c, qq], dev)

    def gather(c, r):
        qq, dev = chip_at(r)
        return copy(full.at[c, core, q], full.at[c, core, q], p3s.at[c, qq], p3r.at[c, core, q], dev)

    def arrived3(c, r):
        qq, dev = chip_at(r)
        return copy(full.at[c, core, qq], full.at[c, core, qq], p3s.at[c, qq], p3r.at[c, core, qq], dev)

    def forward(c, qq):
        return copy(full.at[c, core, qq], full.at[c, core, qq], p4s.at[c, qq], p3r.at[c, core, qq], partner)

    def arrived4(c, qq):
        return copy(full.at[c, other, qq], full.at[c, other, qq], p4s.at[c, qq], p3r.at[c, other, qq], partner)

    def score(stop, j, c):
        k = order_ref[stop, 0, j]
        e = ebuf[stop, c]
        s = jnp.dot(e.astype(jnp.bfloat16), geno_ref[k], preferred_element_type=jnp.float32)
        sq = e * e
        width = sq.shape[1] // lanes
        tot = sq[:, :lanes]
        for i in range(1, width):
            tot = tot + sq[:, i * lanes : (i + 1) * lanes]
        for d in range(2 * quads):
            rg, lb = d // lane_blocks, d % lane_blocks
            sg = d % sq_groups
            part[c, d // quads, d % quads, :rows, :] = s[
                rg * rows : (rg + 1) * rows, lb * lanes : (lb + 1) * lanes
            ]
            part[c, d // quads, d % quads, rows:, :] = tot[sg * sq_rows : (sg + 1) * sq_rows]
        pair(c).start()

    def phase_a(stop, c):
        @pl.when(stop > 0)
        def _():
            hop(stop - 1, c).wait()

        score(stop, 0, c)

    def phase_b(stop, c):
        pair(c).wait()
        part[c, core] = part[c, core] + r1[c]
        for r in range(1, quads):
            spread_out(c, r).start()

    def phase_c(stop, c):
        tot = part[c, core, q]
        for r in range(1, quads):
            arrived2(c, r).wait_recv()
            tot = tot + r2[c, lax.rem(q + r, quads)]
        full[c, core, q] = tot
        for r in range(1, quads):
            gather(c, r).start()
        forward(c, q).start()
        for r in range(1, quads):
            spread_out(c, r).wait_send()

    def phase_d(stop, c):
        for r in range(1, quads):
            arrived3(c, r).wait_recv()
            forward(c, lax.rem(q + r, quads)).start()
        for r in range(1, quads):
            gather(c, r).wait_send()

    def phase_e(stop, j, c):
        for r in range(quads):
            arrived4(c, r).wait_recv()
            forward(c, r).wait_send()
        k = order_ref[stop, 0, j]
        for d in range(2 * quads):
            rg, lb = d // lane_blocks, d % lane_blocks
            scaled[rg * rows : (rg + 1) * rows, lb * lanes : (lb + 1) * lanes] = (
                full[c, d // quads, d % quads, :rows, :] * (1.0 / count)
            ).astype(jnp.bfloat16)
        sq = jnp.concatenate(
            [full[c, g // quads, g % quads, rows:, :] for g in range(sq_groups)], axis=0
        )
        spread = jnp.sum(sq, axis=1, keepdims=True) * (1.0 / count)
        root = jnp.sqrt((spread + epsilon) * (1.0 / count))
        mean = lax.dot_general(scaled[...], inv_ref[k], NT, preferred_element_type=jnp.float32)
        change = mean + (root * droot_ref[k]) * noise_ref[stop, j, c].astype(jnp.float32)
        if j == 0:
            stash[c, 0] = change
        else:
            stash[c, 1] = change
            first = order_ref[stop, 0, 0]
            change_ref[stop, 0, c] = stash[c, first]
            change_ref[stop, 1, c] = stash[c, 1 - first]
        ebuf[stop, c] = ebuf[stop, c] - lax.dot_general(
            change.astype(jnp.bfloat16), geno_ref[k], NT, preferred_element_type=jnp.float32
        )

    total = stops * chunks

    def at(x, fn):
        @pl.when(jnp.logical_and(x >= 0, x < total))
        def _():
            fn(lax.div(x, chunks), lax.rem(x, chunks))

    def last(stop, c):
        phase_e(stop, 1, c)
        hop(stop, c).start()

    def middle(stop, c):
        phase_e(stop, 0, c)
        score(stop, 1, c)

    def body(t, carry):
        at(t - 3, last)
        at(t, phase_a)
        at(t - 1, phase_d)
        at(t - 2, phase_c)
        at(t, phase_b)
        at(t - 1, middle)
        at(t - 2, phase_d)
        at(t, phase_c)
        at(t - 1, phase_b)
        return carry

    lax.fori_loop(0, total + 3, body, 0)
    for c in range(chunks):
        hop(stops - 1, c).wait()
        after_ref[c] = ebuf[stops, c]


def local(mesh_shape, genotypes, residual, posterior_inverse, gibbs_noise, visit_order):
    n_ind, n_mark, n_chip = mesh_shape
    quads = n_ind // 2 * n_chip
    people, traits = residual.shape
    count = people * n_ind * n_chip
    blocks, block = posterior_inverse.shape[:2]
    stops = gibbs_noise.shape[0]
    chunks = CHUNKS
    tc = traits // chunks
    slices = 2 * quads
    lanes = block // min(slices, block // 128)
    rows = tc * (block // lanes) // slices
    sq_rows = max(8, tc // slices)
    f32 = jnp.float32
    geno = genotypes.reshape(people, blocks, block).transpose(1, 0, 2)
    resid = residual.T.reshape(chunks, tc, people)
    noise = gibbs_noise.reshape(stops, blocks, block, traits).transpose(0, 1, 3, 2)
    noise = noise.reshape(stops, blocks, chunks, tc, block)
    droot = jnp.sqrt(jnp.diagonal(posterior_inverse, axis1=1, axis2=2).astype(f32))[:, None, :]
    cfg = (n_ind, n_mark, n_chip, chunks, stops, count, block, rows, lanes, sq_rows)
    vmem = pl.BlockSpec(memory_space=pltpu.VMEM)
    dma = pltpu.SemaphoreType.DMA
    after, changes = pl.pallas_call(
        functools.partial(kernel, cfg),
        out_shape=(
            jax.ShapeDtypeStruct((chunks, tc, people), f32),
            jax.ShapeDtypeStruct((stops, blocks, chunks, tc, block), f32),
        ),
        in_specs=[pl.BlockSpec(memory_space=pltpu.SMEM)] + [vmem] * 5,
        out_specs=(vmem, vmem),
        scratch_shapes=[
            pltpu.VMEM((stops + 1, chunks, tc, people), f32),
            pltpu.VMEM((chunks, 2, quads, rows + sq_rows, lanes), f32),
            pltpu.VMEM((chunks, quads, rows + sq_rows, lanes), f32),
            pltpu.VMEM((chunks, quads, rows + sq_rows, lanes), f32),
            pltpu.VMEM((chunks, 2, quads, rows + sq_rows, lanes), f32),
            pltpu.VMEM((tc, block), jnp.bfloat16),
            pltpu.VMEM((chunks, blocks, tc, block), f32),
            dma((chunks,)),
            dma((chunks,)),
            dma((chunks, quads)),
            dma((chunks, quads)),
            dma((chunks, quads)),
            dma((chunks, 2, quads)),
            dma((chunks, quads)),
            dma((stops, chunks)),
            dma((stops, chunks)),
        ],
        compiler_params=pltpu.CompilerParams(
            collective_id=0, has_side_effects=True, vmem_limit_bytes=56 * 1024 * 1024
        ),
    )(visit_order, geno, resid, posterior_inverse, droot, noise)
    after = after.reshape(traits, people).T
    changes = changes.reshape(stops, blocks, traits, block).transpose(0, 1, 3, 2)
    return after, changes.reshape(stops, blocks * block, traits)


def solution(mesh):
    in_specs = (
        P(("ind", "chip"), "mark"),
        P(("ind", "chip"), "mark"),
        P("mark", None, None),
        P(None, "mark", None),
        P(None, "mark", None),
    )
    out_specs = (P(("ind", "chip"), "mark"), P(None, "mark", None))
    shape = (mesh.shape["ind"], mesh.shape["mark"], mesh.shape["chip"])
    return jax.shard_map(
        functools.partial(local, shape), mesh=mesh, in_specs=in_specs, out_specs=out_specs, check_vma=False
    )
```

```python
import functools

import jax
import jax.numpy as jnp
from jax import lax
from jax.experimental import pallas as pl
from jax.experimental.pallas import tpu as pltpu
from jax.sharding import PartitionSpec as P

epsilon = 1e-05
MESH = pl.DeviceIdType.MESH
CHUNKS = 4
NT = (((1,), (1,)), ((), ()))


def kernel(
    cfg,
    order_ref,
    geno_hbm,
    resid_hbm,
    inv_hbm,
    noise_hbm,
    after_hbm,
    change_hbm,
    geno_ref,
    resid_ref,
    inv_ref,
    noise_raw,
    noise_ref,
    droot_ref,
    change_ref,
    ebuf,
    part,
    r1,
    r2,
    full,
    scaled,
    stash,
    in_sem,
    out_sem,
    after_sem,
    p1s,
    p1r,
    p2s,
    p2r,
    p3s,
    p3r,
    p4s,
    zs,
    zr,
):
    n_ind, n_mark, n_chip, chunks, stops, count, block, rows, lanes, sq_rows = cfg
    quads = n_ind // 2 * n_chip
    tc = ebuf.shape[2]
    lane_blocks = block // lanes
    sq_groups = tc // sq_rows
    ind = lax.axis_index("ind")
    mark = lax.axis_index("mark")
    y = lax.axis_index("chip")
    core = lax.rem(ind, 2)
    other = 1 - core
    q = lax.div(ind, 2) * n_chip + y
    partner = {"ind": ind + 1 - 2 * core}
    nxt = {"mark": lax.rem(mark + 1, n_mark)}
    prv = {"mark": lax.rem(mark + n_mark - 1, n_mark)}

    def chip_at(r):
        qq = lax.rem(q + r, quads)
        return qq, {"ind": lax.div(qq, n_chip) * 2 + core, "chip": lax.rem(qq, n_chip)}

    blocks = geno_ref.shape[0]
    per_visit = chunks // blocks
    piece = noise_ref.shape[3]
    loads = [pltpu.make_async_copy(resid_hbm, resid_ref, in_sem.at[0])]
    for k in range(blocks):
        loads.append(
            pltpu.make_async_copy(
                geno_hbm.at[:, k * block : (k + 1) * block], geno_ref.at[k], in_sem.at[1 + k]
            )
        )
    loads.append(pltpu.make_async_copy(noise_hbm, noise_raw, in_sem.at[1 + blocks]))
    loads.append(pltpu.make_async_copy(inv_hbm, inv_ref, in_sem.at[2 + blocks]))
    for load in loads:
        load.start()

    barrier = pltpu.get_barrier_semaphore()
    pl.semaphore_signal(barrier, inc=1, device_id=partner, device_id_type=MESH)
    pl.semaphore_signal(barrier, inc=1, device_id=nxt, device_id_type=MESH)
    pl.semaphore_signal(barrier, inc=1, device_id=prv, device_id_type=MESH)
    for r in range(1, quads):
        pl.semaphore_signal(barrier, inc=1, device_id=chip_at(r)[1], device_id_type=MESH)

    loads[0].wait()
    flipped = resid_ref[...].T
    for c in range(chunks):
        ebuf[0, c] = flipped[c * tc : (c + 1) * tc]
    for k in range(blocks):
        loads[1 + k].wait()
    pl.semaphore_wait(barrier, quads + 2)

    def copy(src, dst, ssem, rsem, dev):
        return pltpu.make_async_remote_copy(
            src_ref=src, dst_ref=dst, send_sem=ssem, recv_sem=rsem, device_id=dev, device_id_type=MESH
        )

    def hop(stop, c):
        return copy(ebuf.at[stop, c], ebuf.at[stop + 1, c], zs.at[stop, c], zr.at[stop, c], nxt)

    def pair(c):
        return copy(part.at[c, other], r1.at[c], p1s.at[c], p1r.at[c], partner)

    def spread_out(c, r):
        qq, dev = chip_at(r)
        return copy(part.at[c, core, qq], r2.at[c, q], p2s.at[c, qq], p2r.at[c, q], dev)

    def arrived2(c, r):
        qq, dev = chip_at(r)
        return copy(part.at[c, core, qq], r2.at[c, qq], p2s.at[c, qq], p2r.at[c, qq], dev)

    def gather(c, r):
        qq, dev = chip_at(r)
        return copy(full.at[c, core, q], full.at[c, core, q], p3s.at[c, qq], p3r.at[c, core, q], dev)

    def arrived3(c, r):
        qq, dev = chip_at(r)
        return copy(full.at[c, core, qq], full.at[c, core, qq], p3s.at[c, qq], p3r.at[c, core, qq], dev)

    def forward(c, qq):
        return copy(full.at[c, core, qq], full.at[c, core, qq], p4s.at[c, qq], p3r.at[c, core, qq], partner)

    def arrived4(c, qq):
        return copy(full.at[c, other, qq], full.at[c, other, qq], p4s.at[c, qq], p3r.at[c, other, qq], partner)

    def score(stop, j, c):
        k = order_ref[stop, 0, j]
        e = ebuf[stop, c]
        s = jnp.dot(e.astype(jnp.bfloat16), geno_ref[k], preferred_element_type=jnp.float32)
        sq = e * e
        width = sq.shape[1] // lanes
        tot = sq[:, :lanes]
        for i in range(1, width):
            tot = tot + sq[:, i * lanes : (i + 1) * lanes]
        for d in range(2 * quads):
            rg, lb = d // lane_blocks, d % lane_blocks
            sg = d % sq_groups
            part[c, d // quads, d % quads, :rows, :] = s[
                rg * rows : (rg + 1) * rows, lb * lanes : (lb + 1) * lanes
            ]
            part[c, d // quads, d % quads, rows:, :] = tot[sg * sq_rows : (sg + 1) * sq_rows]
        pair(c).start()

    def phase_a(stop, c):
        @pl.when(stop > 0)
        def _():
            hop(stop - 1, c).wait()

        score(stop, 0, c)

    def phase_b(stop, c):
        pair(c).wait()
        part[c, core] = part[c, core] + r1[c]
        for r in range(1, quads):
            spread_out(c, r).start()

    def phase_c(stop, c):
        tot = part[c, core, q]
        for r in range(1, quads):
            arrived2(c, r).wait_recv()
            tot = tot + r2[c, lax.rem(q + r, quads)]
        full[c, core, q] = tot
        for r in range(1, quads):
            gather(c, r).start()
        forward(c, q).start()
        for r in range(1, quads):
            spread_out(c, r).wait_send()

    def phase_d(stop, c):
        for r in range(1, quads):
            arrived3(c, r).wait_recv()
            forward(c, lax.rem(q + r, quads)).start()
        for r in range(1, quads):
            gather(c, r).wait_send()

    def phase_e(stop, j, c):
        for r in range(quads):
            arrived4(c, r).wait_recv()
            forward(c, r).wait_send()
        k = order_ref[stop, 0, j]
        for d in range(2 * quads):
            rg, lb = d // lane_blocks, d % lane_blocks
            scaled[rg * rows : (rg + 1) * rows, lb * lanes : (lb + 1) * lanes] = (
                full[c, d // quads, d % quads, :rows, :] * (1.0 / count)
            ).astype(jnp.bfloat16)
        sq = jnp.concatenate(
            [full[c, g // quads, g % quads, rows:, :] for g in range(sq_groups)], axis=0
        )
        spread = jnp.sum(sq, axis=1, keepdims=True) * (1.0 / count)
        root = jnp.sqrt((spread + epsilon) * (1.0 / count))
        mean = lax.dot_general(scaled[...], inv_ref[k], NT, preferred_element_type=jnp.float32)
        noise = jnp.concatenate(
            [
                noise_ref[stop, j * per_visit + i, pl.ds(pl.multiple_of(c * tc, tc), tc), :]
                for i in range(per_visit)
            ],
            axis=1,
        ).astype(jnp.float32)
        change = mean + (root * droot_ref[k]) * noise
        if j == 0:
            stash[c, 0] = change
        else:
            stash[c, 1] = change
            first = order_ref[stop, 0, 0]
            change_ref[stop, 0, c] = stash[c, first]
            change_ref[stop, 1, c] = stash[c, 1 - first]
        ebuf[stop, c] = ebuf[stop, c] - lax.dot_general(
            change.astype(jnp.bfloat16), geno_ref[k], NT, preferred_element_type=jnp.float32
        )

    total = stops * chunks

    def at(x, fn):
        @pl.when(jnp.logical_and(x >= 0, x < total))
        def _():
            fn(lax.div(x, chunks), lax.rem(x, chunks))

    def out_copy(stop, c):
        return pltpu.make_async_copy(change_ref.at[stop, :, c], change_hbm.at[stop, :, c], out_sem.at[stop, c])

    def last(stop, c):
        phase_e(stop, 1, c)
        hop(stop, c).start()
        out_copy(stop, c).start()

    def flip(stop, i):
        noise_ref[stop, i] = noise_raw[stop, pl.ds(pl.multiple_of(i * piece, piece), piece), :].T

    def prepare():
        loads[1 + blocks].wait()
        lax.fori_loop(0, chunks, lambda i, x: (flip(0, i), x)[1], 0)
        loads[2 + blocks].wait()
        eye = lax.broadcasted_iota(jnp.int32, (128, 128), 0) == lax.broadcasted_iota(
            jnp.int32, (128, 128), 1
        )
        for k in range(blocks):
            for i in range(0, block, 128):
                tile = inv_ref[k, i : i + 128, i : i + 128].astype(jnp.float32)
                diag = jnp.sum(jnp.where(eye, tile, 0.0), axis=0, keepdims=True)
                droot_ref[k, :, i : i + 128] = jnp.sqrt(diag)

    def middle(stop, c):
        phase_e(stop, 0, c)
        score(stop, 1, c)

    def body(t, carry):
        at(t - 3, last)
        at(t, phase_a)
        at(t - 1, phase_d)
        at(t - 2, phase_c)
        pl.when(t == 0)(prepare)
        at(t, phase_b)
        at(t + chunks, flip)
        at(t - 1, middle)
        at(t - 2, phase_d)
        at(t, phase_c)
        at(t - 1, phase_b)
        return carry

    lax.fori_loop(0, total + 3, body, 0)
    def finish(c):
        return pltpu.make_async_copy(ebuf.at[stops, c], after_hbm.at[c], after_sem.at[c])

    for c in range(chunks):
        hop(stops - 1, c).wait()
        finish(c).start()
    for c in range(chunks):
        for stop in range(stops):
            out_copy(stop, c).wait()
        finish(c).wait()


def local(mesh_shape, genotypes, residual, posterior_inverse, gibbs_noise, visit_order):
    n_ind, n_mark, n_chip = mesh_shape
    quads = n_ind // 2 * n_chip
    people, traits = residual.shape
    count = people * n_ind * n_chip
    blocks, block = posterior_inverse.shape[:2]
    stops = gibbs_noise.shape[0]
    chunks = CHUNKS
    tc = traits // chunks
    slices = 2 * quads
    lanes = block // min(slices, block // 128)
    rows = tc * (block // lanes) // slices
    sq_rows = max(8, tc // slices)
    f32 = jnp.float32
    cfg = (n_ind, n_mark, n_chip, chunks, stops, count, block, rows, lanes, sq_rows)
    hbm = pl.BlockSpec(memory_space=pl.ANY)
    dma = pltpu.SemaphoreType.DMA
    after, changes = pl.pallas_call(
        functools.partial(kernel, cfg),
        out_shape=(
            jax.ShapeDtypeStruct((chunks, tc, people), f32),
            jax.ShapeDtypeStruct((stops, blocks, chunks, tc, block), f32),
        ),
        in_specs=[pl.BlockSpec(memory_space=pltpu.SMEM)] + [hbm] * 4,
        out_specs=(hbm, hbm),
        scratch_shapes=[
            pltpu.VMEM((blocks, people, block), jnp.bfloat16),
            pltpu.VMEM((people, traits), f32),
            pltpu.VMEM((blocks, block, block), jnp.bfloat16),
            pltpu.VMEM((stops, blocks * block, traits), jnp.bfloat16),
            pltpu.VMEM((stops, chunks, traits, blocks * block // chunks), jnp.bfloat16),
            pltpu.VMEM((blocks, 1, block), f32),
            pltpu.VMEM((stops, blocks, chunks, tc, block), f32),
            pltpu.VMEM((stops + 1, chunks, tc, people), f32),
            pltpu.VMEM((chunks, 2, quads, rows + sq_rows, lanes), f32),
            pltpu.VMEM((chunks, quads, rows + sq_rows, lanes), f32),
            pltpu.VMEM((chunks, quads, rows + sq_rows, lanes), f32),
            pltpu.VMEM((chunks, 2, quads, rows + sq_rows, lanes), f32),
            pltpu.VMEM((tc, block), jnp.bfloat16),
            pltpu.VMEM((chunks, blocks, tc, block), f32),
            dma((3 + blocks,)),
            dma((stops, chunks)),
            dma((chunks,)),
            dma((chunks,)),
            dma((chunks,)),
            dma((chunks, quads)),
            dma((chunks, quads)),
            dma((chunks, quads)),
            dma((chunks, 2, quads)),
            dma((chunks, quads)),
            dma((stops, chunks)),
            dma((stops, chunks)),
        ],
        compiler_params=pltpu.CompilerParams(
            collective_id=0, has_side_effects=True, vmem_limit_bytes=56 * 1024 * 1024
        ),
    )(visit_order, genotypes, residual, posterior_inverse, gibbs_noise)
    after = after.reshape(traits, people).T
    changes = changes.reshape(stops, blocks, traits, block).transpose(0, 1, 3, 2)
    return after, changes.reshape(stops, blocks * block, traits)


def solution(mesh):
    in_specs = (
        P(("ind", "chip"), "mark"),
        P(("ind", "chip"), "mark"),
        P("mark", None, None),
        P(None, "mark", None),
        P(None, "mark", None),
    )
    out_specs = (P(("ind", "chip"), "mark"), P(None, "mark", None))
    shape = (mesh.shape["ind"], mesh.shape["mark"], mesh.shape["chip"])
    return jax.shard_map(
        functools.partial(local, shape), mesh=mesh, in_specs=in_specs, out_specs=out_specs, check_vma=False
    )
```

```python
import functools

import jax
import jax.numpy as jnp
from jax import lax
from jax.experimental import pallas as pl
from jax.experimental.pallas import tpu as pltpu
from jax.sharding import PartitionSpec as P

epsilon = 1e-05
MESH = pl.DeviceIdType.MESH
CHUNKS = 4
PERIOD = 6
ORDER = (
    ("m", 3),
    ("c", 4),
    ("l", 5),
    ("d", 2),
    ("b", 3),
    ("a", 0),
    ("c", 1),
    ("d", 4),
    ("b", 0),
)
NT = (((1,), (1,)), ((), ()))


def kernel(
    cfg,
    order_ref,
    geno_hbm,
    resid_hbm,
    inv_hbm,
    noise_hbm,
    after_hbm,
    change_hbm,
    geno_ref,
    resid_ref,
    inv_ref,
    noise_raw,
    noise_ref,
    droot_ref,
    change_ref,
    ebuf,
    part,
    r1,
    r2,
    full,
    scaled,
    stash,
    in_sem,
    out_sem,
    after_sem,
    p1s,
    p1r,
    p2s,
    p2r,
    p3s,
    p3r,
    p4s,
    zs,
    zr,
):
    n_ind, n_mark, n_chip, chunks, stops, count, block, rows, lanes, sq_rows = cfg
    quads = n_ind // 2 * n_chip
    tc = ebuf.shape[2]
    lane_blocks = block // lanes
    sq_groups = tc // sq_rows
    ind = lax.axis_index("ind")
    mark = lax.axis_index("mark")
    y = lax.axis_index("chip")
    core = lax.rem(ind, 2)
    other = 1 - core
    q = lax.div(ind, 2) * n_chip + y
    partner = {"ind": ind + 1 - 2 * core}
    nxt = {"mark": lax.rem(mark + 1, n_mark)}
    prv = {"mark": lax.rem(mark + n_mark - 1, n_mark)}

    x_chips = n_ind // 2
    steps = [(dx, dy) for dx in range(x_chips) for dy in range(n_chip)][1:]
    steps.sort(key=lambda d: min(d[0], x_chips - d[0]) + min(d[1], n_chip - d[1]))

    def chip_at(r):
        xx = lax.rem(lax.div(ind, 2) + steps[r - 1][0], x_chips)
        yy = lax.rem(y + steps[r - 1][1], n_chip)
        return xx * n_chip + yy, {"ind": xx * 2 + core, "chip": yy}

    blocks = geno_ref.shape[0]
    per_visit = chunks // blocks
    piece = noise_ref.shape[3]
    loads = [pltpu.make_async_copy(resid_hbm, resid_ref, in_sem.at[0])]
    for k in range(blocks):
        loads.append(
            pltpu.make_async_copy(
                geno_hbm.at[:, k * block : (k + 1) * block], geno_ref.at[k], in_sem.at[1 + k]
            )
        )
    loads.append(pltpu.make_async_copy(noise_hbm, noise_raw, in_sem.at[1 + blocks]))
    loads.append(pltpu.make_async_copy(inv_hbm, inv_ref, in_sem.at[2 + blocks]))
    for load in loads:
        load.start()

    barrier = pltpu.get_barrier_semaphore()
    pl.semaphore_signal(barrier, inc=1, device_id=partner, device_id_type=MESH)
    pl.semaphore_signal(barrier, inc=1, device_id=nxt, device_id_type=MESH)
    pl.semaphore_signal(barrier, inc=1, device_id=prv, device_id_type=MESH)
    for r in range(1, quads):
        pl.semaphore_signal(barrier, inc=1, device_id=chip_at(r)[1], device_id_type=MESH)

    loads[0].wait()
    flipped = resid_ref[...].T
    for c in range(chunks):
        ebuf[0, c] = flipped[c * tc : (c + 1) * tc]
    for k in range(blocks):
        loads[1 + k].wait()
    pl.semaphore_wait(barrier, quads + 2)

    def copy(src, dst, ssem, rsem, dev):
        return pltpu.make_async_remote_copy(
            src_ref=src, dst_ref=dst, send_sem=ssem, recv_sem=rsem, device_id=dev, device_id_type=MESH
        )

    def hop(stop, c):
        return copy(ebuf.at[stop, c], ebuf.at[stop + 1, c], zs.at[stop, c], zr.at[stop, c], nxt)

    def pair(c):
        return copy(part.at[c, other], r1.at[c], p1s.at[c], p1r.at[c], partner)

    def spread_out(c, r):
        qq, dev = chip_at(r)
        return copy(part.at[c, core, qq], r2.at[c, q], p2s.at[c, qq], p2r.at[c, q], dev)

    def arrived2(c, r):
        qq, dev = chip_at(r)
        return copy(part.at[c, core, qq], r2.at[c, qq], p2s.at[c, qq], p2r.at[c, qq], dev)

    def gather(c, r):
        qq, dev = chip_at(r)
        return copy(full.at[c, core, q], full.at[c, core, q], p3s.at[c, qq], p3r.at[c, core, q], dev)

    def arrived3(c, r):
        qq, dev = chip_at(r)
        return copy(full.at[c, core, qq], full.at[c, core, qq], p3s.at[c, qq], p3r.at[c, core, qq], dev)

    def forward(c, qq):
        return copy(full.at[c, core, qq], full.at[c, core, qq], p4s.at[c, qq], p3r.at[c, core, qq], partner)

    def arrived4(c, qq):
        return copy(full.at[c, other, qq], full.at[c, other, qq], p4s.at[c, qq], p3r.at[c, other, qq], partner)

    def score(stop, j, c):
        k = order_ref[stop, 0, j]
        e = ebuf[stop, c]
        s = jnp.dot(e.astype(jnp.bfloat16), geno_ref[k], preferred_element_type=jnp.float32)
        sq = e * e
        width = sq.shape[1] // lanes
        tot = sq[:, :lanes]
        for i in range(1, width):
            tot = tot + sq[:, i * lanes : (i + 1) * lanes]
        for d in range(2 * quads):
            rg, lb = d // lane_blocks, d % lane_blocks
            sg = d % sq_groups
            part[c, d // quads, d % quads, :rows, :] = s[
                rg * rows : (rg + 1) * rows, lb * lanes : (lb + 1) * lanes
            ]
            part[c, d // quads, d % quads, rows:, :] = tot[sg * sq_rows : (sg + 1) * sq_rows]
        pair(c).start()

    def phase_a(stop, c):
        @pl.when(stop > 0)
        def _():
            hop(stop - 1, c).wait()

        score(stop, 0, c)

    def phase_b(stop, c):
        pair(c).wait()
        part[c, core] = part[c, core] + r1[c]
        for r in reversed(range(1, quads)):
            spread_out(c, r).start()

    def phase_c(stop, c):
        tot = part[c, core, q]
        for r in range(1, quads):
            arrived2(c, r).wait_recv()
            tot = tot + r2[c, chip_at(r)[0]]
        full[c, core, q] = tot
        for r in reversed(range(1, quads)):
            gather(c, r).start()
        forward(c, q).start()
        for r in range(1, quads):
            spread_out(c, r).wait_send()

    def phase_d(stop, c):
        for r in range(1, quads):
            arrived3(c, r).wait_recv()
            forward(c, chip_at(r)[0]).start()
        for r in range(1, quads):
            gather(c, r).wait_send()

    def phase_e(stop, j, c):
        for r in range(quads):
            arrived4(c, r).wait_recv()
            forward(c, r).wait_send()
        k = order_ref[stop, 0, j]
        for d in range(2 * quads):
            rg, lb = d // lane_blocks, d % lane_blocks
            scaled[rg * rows : (rg + 1) * rows, lb * lanes : (lb + 1) * lanes] = (
                full[c, d // quads, d % quads, :rows, :] * (1.0 / count)
            ).astype(jnp.bfloat16)
        sq = jnp.concatenate(
            [full[c, g // quads, g % quads, rows:, :] for g in range(sq_groups)], axis=0
        )
        spread = jnp.sum(sq, axis=1, keepdims=True) * (1.0 / count)
        root = jnp.sqrt((spread + epsilon) * (1.0 / count))
        mean = lax.dot_general(scaled[...], inv_ref[k], NT, preferred_element_type=jnp.float32)
        noise = jnp.concatenate(
            [
                noise_ref[stop, j * per_visit + i, pl.ds(pl.multiple_of(c * tc, tc), tc), :]
                for i in range(per_visit)
            ],
            axis=1,
        ).astype(jnp.float32)
        change = mean + (root * droot_ref[k]) * noise
        if j == 0:
            stash[c, 0] = change
        else:
            stash[c, 1] = change
            first = order_ref[stop, 0, 0]
            change_ref[stop, 0, c] = stash[c, first]
            change_ref[stop, 1, c] = stash[c, 1 - first]
        ebuf[stop, c] = ebuf[stop, c] - lax.dot_general(
            change.astype(jnp.bfloat16), geno_ref[k], NT, preferred_element_type=jnp.float32
        )

    def at(x, fn):
        stop, c = lax.div(x, PERIOD), lax.rem(x, PERIOD)

        @pl.when((x >= 0) & (c < chunks) & (stop < stops))
        def _():
            fn(stop, c)

    def out_copy(stop, c):
        return pltpu.make_async_copy(change_ref.at[stop, :, c], change_hbm.at[stop, :, c], out_sem.at[stop, c])

    def last(stop, c):
        phase_e(stop, 1, c)
        hop(stop, c).start()
        out_copy(stop, c).start()

    def flip(stop, i):
        noise_ref[stop, i] = noise_raw[stop, pl.ds(pl.multiple_of(i * piece, piece), piece), :].T

    def prepare():
        loads[1 + blocks].wait()
        lax.fori_loop(0, chunks, lambda i, x: (flip(0, i), x)[1], 0)
        loads[2 + blocks].wait()
        eye = lax.broadcasted_iota(jnp.int32, (128, 128), 0) == lax.broadcasted_iota(
            jnp.int32, (128, 128), 1
        )
        for k in range(blocks):
            for i in range(0, block, 128):
                tile = inv_ref[k, i : i + 128, i : i + 128].astype(jnp.float32)
                diag = jnp.sum(jnp.where(eye, tile, 0.0), axis=0, keepdims=True)
                droot_ref[k, :, i : i + 128] = jnp.sqrt(diag)

    def middle(stop, c):
        phase_e(stop, 0, c)
        score(stop, 1, c)

    phases = {
        "a": phase_a,
        "b": phase_b,
        "c": phase_c,
        "d": phase_d,
        "m": middle,
        "l": last,
    }

    def body(t, carry):
        for name, delay in ORDER:
            if name == "b" and delay == 0:
                pl.when(t == 0)(prepare)
            at(t - delay, phases[name])
        at(t + PERIOD, flip)
        return carry

    lax.fori_loop(0, PERIOD * (stops - 1) + chunks + max(delay for _, delay in ORDER), body, 0)
    def finish(c):
        return pltpu.make_async_copy(ebuf.at[stops, c], after_hbm.at[c], after_sem.at[c])

    for c in range(chunks):
        hop(stops - 1, c).wait()
        finish(c).start()
    for c in range(chunks):
        for stop in range(stops):
            out_copy(stop, c).wait()
        finish(c).wait()


def local(mesh_shape, genotypes, residual, posterior_inverse, gibbs_noise, visit_order):
    n_ind, n_mark, n_chip = mesh_shape
    quads = n_ind // 2 * n_chip
    people, traits = residual.shape
    count = people * n_ind * n_chip
    blocks, block = posterior_inverse.shape[:2]
    stops = gibbs_noise.shape[0]
    chunks = CHUNKS
    tc = traits // chunks
    slices = 2 * quads
    lanes = block // min(slices, block // 128)
    rows = tc * (block // lanes) // slices
    sq_rows = max(8, tc // slices)
    f32 = jnp.float32
    cfg = (n_ind, n_mark, n_chip, chunks, stops, count, block, rows, lanes, sq_rows)
    hbm = pl.BlockSpec(memory_space=pl.ANY)
    dma = pltpu.SemaphoreType.DMA
    after, changes = pl.pallas_call(
        functools.partial(kernel, cfg),
        out_shape=(
            jax.ShapeDtypeStruct((chunks, tc, people), f32),
            jax.ShapeDtypeStruct((stops, blocks, chunks, tc, block), f32),
        ),
        in_specs=[pl.BlockSpec(memory_space=pltpu.SMEM)] + [hbm] * 4,
        out_specs=(hbm, hbm),
        scratch_shapes=[
            pltpu.VMEM((blocks, people, block), jnp.bfloat16),
            pltpu.VMEM((people, traits), f32),
            pltpu.VMEM((blocks, block, block), jnp.bfloat16),
            pltpu.VMEM((stops, blocks * block, traits), jnp.bfloat16),
            pltpu.VMEM((stops, chunks, traits, blocks * block // chunks), jnp.bfloat16),
            pltpu.VMEM((blocks, 1, block), f32),
            pltpu.VMEM((stops, blocks, chunks, tc, block), f32),
            pltpu.VMEM((stops + 1, chunks, tc, people), f32),
            pltpu.VMEM((chunks, 2, quads, rows + sq_rows, lanes), f32),
            pltpu.VMEM((chunks, quads, rows + sq_rows, lanes), f32),
            pltpu.VMEM((chunks, quads, rows + sq_rows, lanes), f32),
            pltpu.VMEM((chunks, 2, quads, rows + sq_rows, lanes), f32),
            pltpu.VMEM((tc, block), jnp.bfloat16),
            pltpu.VMEM((chunks, blocks, tc, block), f32),
            dma((3 + blocks,)),
            dma((stops, chunks)),
            dma((chunks,)),
            dma((chunks,)),
            dma((chunks,)),
            dma((chunks, quads)),
            dma((chunks, quads)),
            dma((chunks, quads)),
            dma((chunks, 2, quads)),
            dma((chunks, quads)),
            dma((stops, chunks)),
            dma((stops, chunks)),
        ],
        compiler_params=pltpu.CompilerParams(
            collective_id=0, has_side_effects=True, vmem_limit_bytes=56 * 1024 * 1024
        ),
    )(visit_order, genotypes, residual, posterior_inverse, gibbs_noise)
    after = after.reshape(traits, people).T
    changes = changes.reshape(stops, blocks, traits, block).transpose(0, 1, 3, 2)
    return after, changes.reshape(stops, blocks * block, traits)


def solution(mesh):
    in_specs = (
        P(("ind", "chip"), "mark"),
        P(("ind", "chip"), "mark"),
        P("mark", None, None),
        P(None, "mark", None),
        P(None, "mark", None),
    )
    out_specs = (P(("ind", "chip"), "mark"), P(None, "mark", None))
    shape = (mesh.shape["ind"], mesh.shape["mark"], mesh.shape["chip"])
    return jax.shard_map(
        functools.partial(local, shape), mesh=mesh, in_specs=in_specs, out_specs=out_specs, check_vma=False
    )
```
